32 devices in a mesh: dp: 16 (over z, y, core), tensor: 2 (over x).
Axes of the slice: x: 2, y: 2, z: 4, core: 2. Of those that a mesh axis runs over, the one named last changes fastest.
Arguments:
- tokens: bfloat16 [4096, 1024], P(('dp', 'tensor')), may hold values from -24 to 24, as said below
- segment_ids: int32 [16, 256], P('dp'), may hold values from 0 to 3, never falling along the last dimension, each value on 1 to 128 neighbouring positions
- norm1_gain: float32 [1024], replicated, may hold values from 0.5 to 1.5
- in_proj: bfloat16 [1024, 3, 1024], P('dp', None, 'tensor'), may hold values from -0.1875 to 0.1875
- conv_weight: float32 [3, 1024], replicated, may hold values from -3 to 3
- out_proj: bfloat16 [1024, 1024], P('dp', 'tensor'), may hold values from -0.1875 to 0.1875
- norm2_gain: float32 [1024], replicated, may hold values from 0.5 to 1.5
- gate_up: bfloat16 [1024, 2, 4608], P('dp', None, 'tensor'), may hold values from -0.1875 to 0.1875
- down_proj: bfloat16 [1024, 4608], P('dp', 'tensor'), may hold values from -0.1875 to 0.1875
- cotangent: bfloat16 [4096, 1024], P(('dp', 'tensor')), may hold values from -6 to 6
Outputs:
- block_out: float32 [4096, 1024], P(('dp', 'tensor'))
- grad_tokens: float32 [4096, 1024], P(('dp', 'tensor'))
- grad_norm1: float32 [1024], replicated
- grad_in_proj: float32 [1024, 3, 1024], P('dp', None, 'tensor')
- grad_conv: float32 [3, 1024], replicated
- grad_out_proj: float32 [1024, 1024], P('dp', 'tensor')
- grad_norm2: float32 [1024], replicated
- grad_gate_up: float32 [1024, 2, 4608], P('dp', None, 'tensor')
- grad_down: float32 [1024, 4608], P('dp', 'tensor')
The draws below stay inside these ranges and needn't reach their ends.
Inputs may be any that keep to these rules, and one draw needn't show every extreme that they name: `segment_ids`: along each row the document numbers never fall; each document spans 1 to 128 tokens and one spans exactly 128. `tokens`: real values.
All inputs are finite; a program needn't handle non-finite values.
Results may differ from the reference program's by a relative error of at most 0.009.
Values may be sent and summed in bfloat16 or wider, within the bound.
A program may use at most 128 MiB of HBM per device.

```python
import math
import jax
import jax.numpy as jnp
import numpy as np
from jax import lax

D = 1024
FF = 4608
TOK_DEV = 256
SEGS = 4
MOST_DOC = 128
TOKENS = 4096
N_DP = 16


def draw_tokens(key, part):
    keys = jax.random.split(jax.random.fold_in(key, 11), 3)
    base = jax.random.normal(keys[0], (TOKENS, D), jnp.float32)
    row_scale = jnp.exp(jax.random.uniform(keys[1], (TOKENS, 1), jnp.float32, math.log(0.3), math.log(3.0)))
    col_scale = jnp.exp(jax.random.uniform(keys[2], (1, D), jnp.float32, math.log(0.5), math.log(2.0)))
    return jnp.clip(base * row_scale * col_scale, -24.0, 24.0).astype(jnp.bfloat16)


def with_spikes(values, rng, source, target, parts, factor):
    def block_of(position):
        return (jnp.arange(values.shape[position]) // (values.shape[position] // parts)).reshape((-1,) + (1,) * (values.ndim - 1 - position))

    first = jax.random.permutation(rng, parts)[block_of(target)]
    other_side = (block_of(target) + parts // 2) % parts
    return jnp.where((block_of(source) == first) | (block_of(source) == other_side), factor * values, values)


def shard_levels(stream_key, shape, shards, smallest, high):
    factor_of = 1.0
    for dim, parts in shards:
        draws = jax.random.uniform(jax.random.fold_in(jax.random.fold_in(stream_key, 6), dim), (parts,), jnp.float32, smallest / len(shards), high / len(shards))
        factor_of = factor_of * jnp.repeat(jnp.exp(draws), shape[dim] // parts).reshape((-1,) + (1,) * (len(shape) - 1 - dim))
    return factor_of


def split_up(amount, total, bound, lean):
    weights = [(1 << 20) // math.isqrt(rank ** lean) + 1 for rank in range(2, amount + 1)]
    rest, given = total - bound - (amount - 1), [1] * (amount - 1)
    while rest > 0:
        candidates = [i for i in range(amount - 1) if given[i] < bound]
        mass, remaining = sum([weights[i] for i in candidates]), rest
        for i in candidates:
            extra = min(bound - given[i], max(1, remaining * weights[i] // mass), rest)
            given[i] = given[i] + extra
            rest = rest - extra
    return np.array([bound] + given)


def uneven_parts(key, number_of, total, reach, skew):
    if number_of == 2:
        one = jax.random.randint(key, (), max(1, total - reach), min(reach, total - 1) + 1)
        return jnp.stack([one, total - one])
    sizes = jnp.asarray(split_up(number_of, total, reach, skew), jnp.int32)
    twos = (number_of - 1) // 2
    source_of, taker = sizes[1:1 + 2 * twos:2], sizes[2:2 + 2 * twos:2]
    slack = jnp.minimum(source_of - 1, reach - taker)
    moved = jax.random.randint(jax.random.fold_in(key, 1), (twos,), 0, 1 << 20) % (slack + 1)
    sizes = sizes.at[1:1 + 2 * twos:2].set(source_of - moved).at[2:2 + 2 * twos:2].set(taker + moved)
    return sizes[jax.random.permutation(jax.random.fold_in(key, 2), number_of)]


def bell_draw(rng, dims, scale, bound, cuts=(), held_as=jnp.bfloat16):
    drawn = scale * jax.random.normal(rng, dims, jnp.float32)
    if cuts:
        drawn = drawn * shard_levels(rng, dims, cuts, -0.22, 0.18)
    return jnp.clip(drawn, -bound, bound).astype(held_as)


def bell_draw_with(stream_key, shape, deviation, most, cuts, heavy, kind=jnp.bfloat16):
    values = deviation * jax.random.normal(stream_key, shape, jnp.float32)
    if cuts:
        values = values * shard_levels(stream_key, shape, cuts, -0.22, 0.18)
    return jnp.clip(with_spikes(values, jax.random.fold_in(stream_key, 3), *heavy), -most, most).astype(kind)


def setup_inputs(seed: int = 0) -> dict:
    arg_keys = jax.random.split(jax.random.key(seed), 11)
    return {
        "tokens": draw_tokens(jax.random.fold_in(arg_keys[10], 71), 0),
        "segment_ids": jax.vmap(lambda own: jnp.searchsorted(jnp.cumsum(uneven_parts(own, SEGS, TOK_DEV, MOST_DOC, 1)), jnp.arange(TOK_DEV), side="right"))(jax.random.split(arg_keys[1], N_DP)).reshape((N_DP, TOK_DEV)).astype(jnp.int32),
        "norm1_gain": jnp.clip(1.0 + 0.1 * jax.random.normal(arg_keys[2], (D,), jnp.float32), 0.5, 1.5),
        "in_proj": bell_draw(arg_keys[3], (D, 3, D), D ** -0.5, 0.1875, ((0, 16), (2, 2))),
        "conv_weight": bell_draw(arg_keys[4], (3, D), 0.6, 3.0, (), jnp.float32),
        "out_proj": bell_draw(arg_keys[5], (D, D), D ** -0.5, 0.1875, ((0, 16), (1, 2))),
        "norm2_gain": jnp.clip(1.0 + 0.1 * jax.random.normal(arg_keys[6], (D,), jnp.float32), 0.5, 1.5),
        "gate_up": bell_draw(arg_keys[7], (D, 2, FF), D ** -0.5, 0.1875, ((0, 16), (2, 2))),
        "down_proj": bell_draw(arg_keys[8], (D, FF), (FF // 4) ** -0.5, 0.1875, ((0, 16), (1, 2))),
        "cotangent": bell_draw_with(arg_keys[9], (TOKENS, D), 1.0, 6.0, ((0, 32),), (0, 1, 32, 2.75)),
    }


EPSILON = 1e-05

def matmul(form, left, right):
    return jnp.einsum(form, left.astype(jnp.float32), right.astype(jnp.float32), precision=lax.Precision.HIGHEST)

def rms_forward(values, norm_gain):
    factor = lax.rsqrt(lax.optimization_barrier(jnp.mean(values * values, axis=-1, keepdims=True)) + EPSILON)
    return (values * factor * norm_gain, factor)

def rms_backward(values, factor, norm_gain, upstream):
    scaled = upstream * norm_gain
    result = factor * scaled - values * (factor * factor * factor) * lax.optimization_barrier(jnp.mean(scaled * values, axis=-1, keepdims=True))
    return (result, lax.optimization_barrier(jnp.sum(upstream * values * factor, axis=0)))

def lagged(values, offset):
    return jnp.concatenate([jnp.zeros((offset, values.shape[1]), values.dtype), values[:-offset]], axis=0)

def leading(values, offset):
    return jnp.concatenate([values[offset:], jnp.zeros((offset, values.shape[1]), values.dtype)], axis=0)

def reset_masks(segment):
    same_one = jnp.concatenate([jnp.zeros((1,), jnp.bool_), segment[1:] == segment[:-1]])
    same_two = jnp.concatenate([jnp.zeros((2,), jnp.bool_), segment[2:] == segment[:-2]])
    return (same_one.astype(jnp.float32)[:, None], same_two.astype(jnp.float32)[:, None])

def conv_forward(values, kernel, mask_one, mask_two):
    return kernel[0] * values + kernel[1] * mask_one * lagged(values, 1) + kernel[2] * mask_two * lagged(values, 2)

def conv_backward(values, upstream, kernel, mask_one, mask_two):
    result = kernel[0] * upstream + leading(kernel[1] * mask_one * upstream, 1) + leading(kernel[2] * mask_two * upstream, 2)
    grads = jnp.stack([lax.optimization_barrier(jnp.sum(upstream * values, axis=0)), lax.optimization_barrier(jnp.sum(upstream * mask_one * lagged(values, 1), axis=0)), lax.optimization_barrier(jnp.sum(upstream * mask_two * lagged(values, 2), axis=0))])
    return (result, grads)

def block_pass(seq_tokens, segment, seq_cotangent, norm1_gain, in_proj, conv_weight, out_proj, norm2_gain, gate_up, down_proj):
    inputs = seq_tokens.astype(jnp.float32)
    mask_one, mask_two = reset_masks(segment)
    normed_one, factor_one = rms_forward(inputs, norm1_gain)
    normed_one = normed_one.astype(jnp.bfloat16)
    projected = matmul('td,djc->jtc', normed_one, in_proj)
    b_part, c_part, x_part = (projected[0], projected[1], projected[2])
    mixed_in = b_part * x_part
    conv_out = conv_forward(mixed_in, conv_weight, mask_one, mask_two)
    gated = (c_part * conv_out).astype(jnp.bfloat16)
    resid = inputs + matmul('tc,dc->td', gated, out_proj)
    normed_two, factor_two = rms_forward(resid, norm2_gain)
    normed_two = normed_two.astype(jnp.bfloat16)
    lifted = matmul('td,djf->jtf', normed_two, gate_up)
    gate_lin, up_lin = (lifted[0], lifted[1])
    sigmoid_gate = jax.nn.sigmoid(gate_lin)
    activ = gate_lin * sigmoid_gate
    hidden = (activ * up_lin).astype(jnp.bfloat16)
    block_out = resid + matmul('tf,df->td', hidden, down_proj)
    grad_down = matmul('td,tf->df', seq_cotangent, hidden)
    back_hidden = matmul('td,df->tf', seq_cotangent, down_proj)
    back_gate = (back_hidden * up_lin * sigmoid_gate * (1.0 + gate_lin * (1.0 - sigmoid_gate))).astype(jnp.bfloat16)
    back_up = (back_hidden * activ).astype(jnp.bfloat16)
    back_lifted = jnp.stack([back_gate, back_up])
    grad_gate_up = matmul('td,jtf->djf', normed_two, back_lifted)
    back_normed2 = matmul('jtf,djf->td', back_lifted, gate_up)
    resid_part, grad_norm2 = rms_backward(resid, factor_two, norm2_gain, back_normed2)
    back_resid = seq_cotangent.astype(jnp.float32) + resid_part
    back_resid16 = back_resid.astype(jnp.bfloat16)
    grad_out_proj = matmul('td,tc->dc', back_resid16, gated)
    back_gated = matmul('td,dc->tc', back_resid16, out_proj)
    back_c = back_gated * conv_out
    back_conv = back_gated * c_part
    back_mixed, grad_conv = conv_backward(mixed_in, back_conv, conv_weight, mask_one, mask_two)
    back_proj = jnp.stack([back_mixed * x_part, back_c, back_mixed * b_part]).astype(jnp.bfloat16)
    grad_in_proj = matmul('td,jtc->djc', normed_one, back_proj)
    back_normed1 = matmul('jtc,djc->td', back_proj, in_proj)
    input_part, grad_norm1 = rms_backward(inputs, factor_one, norm1_gain, back_normed1)
    grad_tokens = back_resid + input_part
    return ((block_out, grad_tokens), (grad_norm1, grad_in_proj, grad_conv, grad_out_proj, grad_norm2, grad_gate_up, grad_down))

def reference(tokens, segment_ids, norm1_gain, in_proj, conv_weight, out_proj, norm2_gain, gate_up, down_proj, cotangent):
    blocks = (tokens.reshape(N_DP, TOK_DEV, D), segment_ids, cotangent.reshape(N_DP, TOK_DEV, D))
    start = (jnp.zeros((D,), jnp.float32), jnp.zeros((D, 3, D), jnp.float32), jnp.zeros((3, D), jnp.float32), jnp.zeros((D, D), jnp.float32), jnp.zeros((D,), jnp.float32), jnp.zeros((D, 2, FF), jnp.float32), jnp.zeros((D, FF), jnp.float32))

    def layer_step(totals, inputs):
        seq_tokens, segment, seq_cotangent = inputs
        outputs, grads = block_pass(seq_tokens, segment, seq_cotangent, norm1_gain, in_proj, conv_weight, out_proj, norm2_gain, gate_up, down_proj)
        return (jax.tree.map(lambda first_term, other_term: first_term + other_term, totals, grads), outputs)
    totals, outputs = lax.scan(layer_step, start, blocks)
    block_out = outputs[0].reshape(TOKENS, D)
    grad_tokens = outputs[1].reshape(TOKENS, D)
    return (block_out, grad_tokens, totals[0], totals[1], totals[2], totals[3], totals[4], totals[5], totals[6])
```

```python
import functools
from types import SimpleNamespace

import jax
import jax.numpy as jnp
from jax import lax
from jax.experimental import pallas as pl
from jax.experimental.pallas import tpu as pltpu
from jax.sharding import PartitionSpec as P

EPSILON = 1e-05
MESH = pl.DeviceIdType.MESH
F32, BF16 = jnp.float32, jnp.bfloat16
NN, NT = ((1,), (0,)), ((1,), (1,))


def chip_at(pos, chips):
    back = pos // (chips // 2)
    return (1 - back) * 2 * pos + back * (2 * (chips - 1 - pos) + 1)


def ring_place(chips):
    me = lax.axis_index("dp")
    core, chip = me % 2, me // 2
    odd = chip % 2
    pos = (1 - odd) * (chip // 2) + odd * (chips - 1 - chip // 2)

    def owner(steps):
        return chip_at((pos + steps + 2 * chips) % chips, chips)

    return me, core, chip, owner


def greet(others):
    barrier = pltpu.get_barrier_semaphore()
    peer = 1 - lax.axis_index("tensor")
    pl.semaphore_signal(barrier, inc=1, device_id={"tensor": peer}, device_id_type=MESH)
    for other in others:
        pl.semaphore_signal(barrier, inc=1, device_id={"dp": other}, device_id_type=MESH)
    pl.semaphore_wait(barrier, len(others) + 1)


def mm(left, right, dims):
    return lax.dot_general(left, right, (dims, ((), ())), preferred_element_type=F32)


def flat(block):
    count, rows, cols = block.shape
    if rows % 16:
        return block.astype(F32).reshape(count * rows, cols).astype(BF16)
    return block.reshape(count * rows, cols)


def tile_of(cols):
    return next(t for t in (768, 512, 256) if cols % t == 0)


def span(index, size):
    return pl.ds(pl.multiple_of(index * size, size), size)


def pieces(cols, count):
    tiles = cols // 128
    sizes = [(tiles * (i + 1) // count - tiles * i // count) * 128 for i in range(count)]
    return [(sum(sizes[:i]), sizes[i]) for i in range(count)]


def block_kernel(dims, names, *refs):
    chips, ranks, rows, depth, channels, hidden_units, half = dims
    r = SimpleNamespace(**dict(zip(names, refs)))
    me, core, chip, owner = ring_place(chips)
    partner = chip * 2 + 1 - core
    nexts = {way: owner(way) * 2 + core for way in (1, -1)}
    column = lax.axis_index("tensor") * channels
    per_block = 256 // rows
    blocks = depth // 256
    small_tile = 256
    last = chips - 1
    if not hasattr(r, "s_send"):
        r.s_send, r.s_recv, r.s_hand, r.s_take = r.g_send, r.g_recv, r.g_hand, r.g_take

    def remote(src, dst, send, recv, where):
        return pltpu.make_async_remote_copy(
            src_ref=src,
            dst_ref=dst,
            send_sem=send,
            recv_sem=recv,
            device_id=where,
            device_id_type=MESH,
        )

    gathers = []
    for j, way in ((0, 1), (1, 1), (2, -1)):
        gathers.append((0, way, r.in_sh.at[j], lambda slot, j=j: r.in_full.at[j, slot]))
    gathers.append((0, -1, r.out_sh, lambda slot: r.out_full.at[slot]))
    for way, shard, full in ((1, r.gate_sh, r.gate_full), (-1, r.up_sh, r.up_full)):
        for start, size in pieces(hidden_units, 2):
            cols = pl.ds(start, size)
            gathers.append(
                (1, way, shard.at[:, cols], lambda slot, full=full, cols=cols: full.at[slot, :, cols])
            )
    for k, (start, size) in enumerate(pieces(hidden_units, 4)):
        cols = pl.ds(start, size)
        gathers.append(
            (2, 1 - 2 * (k // 2), r.down_sh.at[:, cols], lambda slot, cols=cols: r.down_full.at[slot, :, cols])
        )
    arriving, unsent, taken, kept = {}, {0: [], 1: [], 2: []}, {0: [], 1: [], 2: []}, {0: [], 1: [], 2: []}

    def gather(group, step):
        for f, (own_group, way, shard, place) in enumerate(gathers):
            if own_group != group:
                continue
            slot = owner(-way * step) * 2 + core
            if step:
                arriving[f].wait_recv()
            source = place(slot) if step else shard
            if step < last:
                ring = remote(
                    source, place(slot), r.g_send.at[f, step], r.g_recv.at[f, step], {"dp": nexts[way]}
                )
                ring.start()
                arriving[f] = ring
                unsent[group].append(ring)
            hand = remote(
                source, place(slot), r.g_hand.at[f, step], r.g_take.at[f, step], {"dp": partner}
            )
            hand.start()
            taken[group].append(hand)
            unsent[group].append(hand)
            if step == 0:
                keep = pltpu.make_async_copy(shard, place(me), r.g_own.at[f])
                keep.start()
                kept[group].append(keep)

    def gathered(group):
        for hand in taken[group]:
            hand.wait_recv()
        for keep in kept[group]:
            keep.wait()

    def sent(group):
        for copy in unsent[group]:
            copy.wait_send()

    def across(index, source, into):
        copy = remote(
            source,
            into,
            r.x_send.at[index],
            r.x_recv.at[index],
            {"tensor": 1 - lax.axis_index("tensor")},
        )
        copy.start()
        return copy

    scatters = []
    for k, (start, size) in enumerate(pieces(hidden_units, 4)):
        way = 1 - 2 * (k // 2)
        scatters.append((0, way, r.grad_down, r.theirs_down, r.moving_down, start, size, r.slope, 0, start))
    for way, grad, theirs, moving, place in (
        (1, r.down_full, r.theirs_gate, r.moving_gate, 1),
        (-1, r.gate_full, r.theirs_up, r.moving_up, 2),
    ):
        for start, size in pieces(hidden_units, 2):
            scatters.append((1, way, grad, theirs, moving, start, size, r.slope, place * rows, start))
    for j, way in ((0, 1), (1, 1), (2, -1), (3, -1)):
        scatters.append(
            (2, way, r.up_full, r.theirs_io, r.moving_io, j * channels, channels, r.activ, j * rows, 0)
        )
    swaps, hops = {}, {}

    def swap(group):
        for step in range(chips):
            for f, (own_group, way, grad, theirs, _, start, size, *_) in enumerate(scatters):
                if own_group != group:
                    continue
                target = owner(-way * (step + 1))
                cols = pl.ds(start, size)
                copy = remote(
                    grad.at[target * 2 + 1 - core, :, cols],
                    theirs.at[step, :, cols],
                    r.s_hand.at[f, step],
                    r.s_take.at[f, step],
                    {"dp": partner},
                )
                copy.start()
                swaps[f, step] = copy

    def scatter(group, step):
        tile = min(rows, 16)
        for f, (own_group, way, grad, theirs, moving, start, size, stage, row, col) in enumerate(scatters):
            if own_group != group:
                continue
            slot = owner(-way * (step + 1)) * 2 + core
            cols = pl.ds(start, size)
            swaps[f, step].wait_recv()
            if step:
                hops[f, step - 1].wait_recv()

            @pl.loop(0, rows // tile)
            def _(block):
                at = span(block, tile)
                total = grad[slot, at, cols].astype(F32) + theirs[step, at, cols].astype(F32)
                if step:
                    total = total + moving[step - 1, at, cols].astype(F32)
                if step == last:
                    stage[pl.ds(pl.multiple_of(row + block * tile, tile), tile), pl.ds(col, size)] = total
                elif step:
                    moving[step - 1, at, cols] = total.astype(BF16)
                else:
                    grad[slot, at, cols] = total.astype(BF16)

            if step < last:
                source = moving.at[step - 1, :, cols] if step else grad.at[slot, :, cols]
                hop = remote(
                    source, moving.at[step, :, cols], r.s_send.at[f, step], r.s_recv.at[f, step], {"dp": nexts[way]}
                )
                hop.start()
                hops[f, step] = hop

    saves = []

    def save(index, source, into):
        copy = pltpu.make_async_copy(source, into, r.o_sem.at[index])
        copy.start()
        saves.append(copy)

    def row_loop(body):
        @pl.loop(0, half // 16)
        def _(index):
            body(span(index, 16))

    def turned(source, into):
        @pl.loop(0, depth // 128)
        def _(index):
            at = span(index, 128)
            into[at, :] = source[:, at].astype(F32).T.astype(BF16)

    def outer(left, right, into, offset, low, high):
        cols = right.shape[1]
        tile = tile_of(cols)

        @pl.loop(low, high)
        def _(block):
            @pl.loop(0, cols // tile)
            def _(n):
                value = mm(left[span(block, 256), :], right[:, span(n, tile)], NN)
                at = pl.ds(pl.multiple_of(offset + n * tile, 128), tile)
                into[span(block, per_block), :, at] = value.reshape(per_block, rows, tile).astype(BF16)

    def factor_of(values):
        return lax.rsqrt(jnp.mean(values * values, axis=-1, keepdims=True) + EPSILON)

    def norm_one(at):
        values = r.tokens[at, :].astype(F32)
        r.rows_one[at, :] = (values * factor_of(values) * r.gain1[...]).astype(BF16)
        r.cot_rows[at, :] = r.cot[at, :]

    def project():
        @pl.loop(0, 3)
        def _(j):
            @pl.loop(0, channels // small_tile)
            def _(n):
                cols = span(n, small_tile)
                r.projected[j, :, cols] = mm(r.rows_one[...], flat(r.in_full[j, :, :, cols]), NN)

    def shifted(values):
        return pltpu.roll(values, 1, 0), pltpu.roll(values, 2, 0)

    def taps(n):
        at = pl.ds(pl.multiple_of(column + n * 128, 128), 128)
        return [r.conv[k : k + 1, at] for k in range(3)], at

    def convolve():
        @pl.loop(0, channels // 128)
        def _(n):
            cols = span(n, 128)
            kernel, _ = taps(n)
            mixed = r.projected[0, :, cols] * r.projected[2, :, cols]
            one, two = shifted(mixed)
            out = kernel[0] * mixed + kernel[1] * (r.masks[0] * one) + kernel[2] * (r.masks[1] * two)
            r.conv_out[:, cols] = out
            r.gated[:, cols] = (r.projected[1, :, cols] * out).astype(BF16)

    def out_terms():
        @pl.loop(0, blocks)
        def _(b):
            value = mm(r.gated[...], flat(r.out_full[span(b, per_block), :, :]), NT)
            at = span(b, 256)
            r.acc[:, at] = value[:half]
            r.away0[:, at] = value[half:].astype(BF16)

    def residual(at):
        values = r.tokens[at, :].astype(F32) + (r.acc[at, :] + r.near0[at, :].astype(F32))
        r.resid[at, :] = values
        r.rows_two[at, :] = (values * factor_of(values) * r.gain2[...]).astype(BF16)

    def gate_up(low, high):
        @pl.loop(low, high)
        def _(n):
            cols = span(n, small_tile)
            gate = mm(r.rows_two[...], flat(r.gate_full[:, :, cols]), NN)
            up = mm(r.rows_two[...], flat(r.up_full[:, :, cols]), NN)
            sigmoid = jax.nn.sigmoid(gate)
            activ = gate * sigmoid
            r.hidden[:, cols] = (activ * up).astype(BF16)
            r.activ[:, cols] = activ
            r.slope[:, cols] = up * sigmoid * (1.0 + gate * (1.0 - sigmoid))

    def back_hidden(low, high):
        @pl.loop(low, high)
        def _(n):
            cols = span(n, small_tile)
            back = mm(r.cot_rows[...], flat(r.down_full[:, :, cols]), NN)
            r.back_gate[:, cols] = (back * r.slope[:, cols]).astype(BF16)
            r.back_up[:, cols] = (back * r.activ[:, cols]).astype(BF16)

    def ffn_terms():
        @pl.loop(0, blocks)
        def _(b):
            value = mm(r.hidden[...], flat(r.down_full[span(b, per_block), :, :]), NT)
            at = span(b, 256)
            r.block_out[:, at] = r.resid[:, at] + value[:half]
            r.away1[:, at] = value[half:].astype(BF16)

    def back_two(low, high):
        @pl.loop(low, high)
        def _(b):
            rows_at = span(b, per_block)
            value = mm(r.back_gate[...], flat(r.gate_full[rows_at, :, :]), NT)
            value = value + mm(r.back_up[...], flat(r.up_full[rows_at, :, :]), NT)
            at = span(b, 256)
            r.acc[:, at] = value[:half]
            r.away2[:, at] = value[half:].astype(BF16)

    def norm_back(values, gain, upstream, small_row):
        factor = factor_of(values)
        scaled = upstream * gain
        mean = jnp.mean(scaled * values, axis=-1, keepdims=True)
        r.small[small_row : small_row + 1, :] += jnp.sum(upstream * values * factor, axis=0, keepdims=True)
        return factor * scaled - values * (factor * factor * factor) * mean

    def residual_back(at):
        upstream = r.acc[at, :] + r.near2[at, :].astype(F32)
        back = r.cot[at, :].astype(F32) + norm_back(r.resid[at, :], r.gain2[...], upstream, 1)
        r.grad_tokens[at, :] = back
        r.resid_rows[at, :] = back.astype(BF16)

    def mixer_back():
        @pl.loop(0, channels // 128)
        def _(n):
            cols = span(n, 128)
            kernel, at = taps(n)
            gated_back = mm(r.resid_rows[...], flat(r.out_full[:, :, cols]), NN)
            b_part, c_part, x_part = [r.projected[j, :, cols] for j in range(3)]
            mixed = b_part * x_part
            one, two = shifted(mixed)
            one, two = r.masks[0] * one, r.masks[1] * two
            conv_back = gated_back * c_part
            mixed_back = (
                kernel[0] * conv_back
                + pltpu.roll(kernel[1] * (r.masks[0] * conv_back), 2 * half - 1, 0)
                + pltpu.roll(kernel[2] * (r.masks[1] * conv_back), 2 * half - 2, 0)
            )
            for k, term in enumerate((mixed, one, two)):
                r.small[2 + k : 3 + k, at] = jnp.sum(conv_back * term, axis=0, keepdims=True)
            r.back_proj[0, :, cols] = (mixed_back * x_part).astype(BF16)
            r.back_proj[1, :, cols] = (gated_back * r.conv_out[:, cols]).astype(BF16)
            r.back_proj[2, :, cols] = (mixed_back * b_part).astype(BF16)

    def back_one():
        @pl.loop(0, blocks)
        def _(b):
            rows_at = span(b, per_block)
            value = mm(r.back_proj[0], flat(r.in_full[0, rows_at, :, :]), NT)
            for j in (1, 2):
                value = value + mm(r.back_proj[j], flat(r.in_full[j, rows_at, :, :]), NT)
            at = span(b, 256)
            r.acc[:, at] = value[:half]
            r.away3[:, at] = value[half:].astype(BF16)

    def tokens_back(at):
        upstream = r.acc[at, :] + r.near3[at, :].astype(F32)
        r.grad_tokens[at, :] += norm_back(r.tokens[at, :].astype(F32), r.gain1[...], upstream, 0)

    small_hops = []

    def small_hop(step):
        slot = owner(-step)
        if step:
            small_hops[step - 1].wait_recv()
        if step < last:
            hop = remote(
                r.smalls.at[slot], r.smalls.at[slot], r.m_send.at[step], r.m_recv.at[step], {"dp": nexts[1]}
            )
            hop.start()
            small_hops.append(hop)

    first, second = pl.ds(0, half), pl.ds(half, half)

    greet((nexts[1], nexts[-1], partner))
    gather(0, 0)
    cot_swap = across(0, r.cot, r.cot_rows.at[second])
    row_loop(norm_one)
    rows_swap = across(1, r.rows_one.at[first], r.rows_one.at[second])
    r.small[...] = jnp.zeros_like(r.small)
    for step in range(1, last):
        gather(0, step)
    gather(1, 0)
    gather(0, last)
    gathered(0)
    rows_swap.wait_recv()
    project()
    convolve()
    out_terms()
    terms_swap = across(2, r.away0, r.near0)
    gather(1, 1)
    cot_swap.wait_recv()
    turned(r.cot_rows, r.across_t)
    mid = max(3, last // 2)
    for step in range(2, mid):
        gather(1, step)
    terms_swap.wait_recv()
    row_loop(residual)
    two_swap = across(3, r.rows_two.at[first], r.rows_two.at[second])
    for step in range(mid, last):
        gather(1, step)
    gather(2, 0)
    gather(1, last)
    gathered(1)
    two_swap.wait_recv()
    tiles = hidden_units // small_tile
    cuts = [tiles * k // 3 for k in range(4)]
    at_step = 1
    for k in range(3):
        gate_up(cuts[k], cuts[k + 1])
        gather(2, at_step)
        at_step += 1
    bounds = [blocks * k // 2 for k in range(3)]
    outer(r.across_t, r.hidden, r.grad_down, 0, bounds[0], bounds[1])
    gather(2, at_step)
    outer(r.across_t, r.hidden, r.grad_down, 0, bounds[1], bounds[2])
    swap(0)
    for step in range(at_step + 1, last):
        gather(2, step)
    turned(r.rows_two, r.across_t)
    scatter(0, 0)
    gather(2, last)
    gathered(2)
    back_hidden(0, tiles)
    scatter(0, 1)
    ffn_terms()
    ffn_swap = across(4, r.away1, r.near1)
    back_two(0, blocks // 2)
    scatter(0, 2)
    back_two(blocks // 2, blocks)
    back_swap = across(5, r.away2, r.near2)
    sent(2)
    outer(r.across_t, r.back_gate, r.down_full, 0, bounds[0], bounds[1])
    scatter(0, 3)
    outer(r.across_t, r.back_gate, r.down_full, 0, bounds[1], bounds[2])
    sent(1)
    outer(r.across_t, r.back_up, r.gate_full, 0, bounds[0], bounds[1])
    scatter(0, 4)
    outer(r.across_t, r.back_up, r.gate_full, 0, bounds[1], bounds[2])
    swap(1)
    back_swap.wait_recv()
    row_loop(residual_back)
    resid_swap = across(6, r.resid_rows.at[first], r.resid_rows.at[second])
    for step in range(5, last):
        scatter(0, step)
    scatter(1, 0)
    scatter(0, last)
    resid_swap.wait_recv()
    mixer_back()
    scatter(1, 1)
    back_one()
    last_swap = across(7, r.away3, r.near3)
    turned(r.rows_one, r.across_t)
    for j in range(3):
        outer(r.across_t, r.back_proj.at[j], r.up_full, j * channels, 0, blocks)
    scatter(1, 2)
    turned(r.resid_rows, r.across_t)
    outer(r.across_t, r.gated, r.up_full, 3 * channels, 0, blocks)
    swap(2)
    scatter(1, 3)
    last_swap.wait_recv()
    row_loop(tokens_back)
    pair = remote(r.small, r.small_pair, r.m_pair.at[0], r.m_pair.at[1], {"dp": partner})
    pair.start()
    ffn_swap.wait_recv()

    @row_loop
    def _(at):
        r.block_out[at, :] += r.near1[at, :].astype(F32)

    for step in range(4, last):
        scatter(1, step)
    scatter(2, 0)
    pair.wait_recv()
    r.smalls[chip] = r.small[...] + r.small_pair[...]
    small_hop(0)
    scatter(1, last)
    for step in range(1, last):
        small_hop(step)
        scatter(2, step)
    small_hop(last)
    r.folded[...] = lax.fori_loop(1, chips, lambda k, total: total + r.smalls[k], r.smalls[0])
    fold_swap = across(8, r.folded, r.folded_other)
    save(0, r.slope.at[pl.ds(0, rows), :], r.o_down)
    save(1, r.slope.at[pl.ds(rows, rows), :], r.o_gate)
    save(2, r.slope.at[pl.ds(2 * rows, rows), :], r.o_up)
    scatter(2, last)
    for j in range(3):
        save(3 + j, r.activ.at[pl.ds(j * rows, rows), pl.ds(0, channels)], r.o_in.at[j])
    save(6, r.activ.at[pl.ds(3 * rows, rows), pl.ds(0, channels)], r.o_out)
    fold_swap.wait_recv()
    r.o_small[...] = r.folded[...] + r.folded_other[...]
    for copy in saves:
        copy.wait()
    sent(0)
    for copy in list(hops.values()) + list(swaps.values()) + small_hops + [pair]:
        copy.wait_send()
    for copy in (
        cot_swap, rows_swap, terms_swap, two_swap, ffn_swap, back_swap, resid_swap, last_swap, fold_swap
    ):
        copy.wait_send()


def run_block(tokens, cot, masks, conv, gain1, gain2, in_sh, out_sh, gate_sh, up_sh, down_sh, ranks):
    chips = ranks // 2
    half, depth = tokens.shape
    rows, channels = out_sh.shape
    units = down_sh.shape[1]
    full = 2 * half
    vmem, dma = pltpu.VMEM, pltpu.SemaphoreType.DMA
    inputs = dict(
        tokens=tokens, cot=cot, masks=masks, conv=conv, gain1=gain1, gain2=gain2,
        in_sh=in_sh, out_sh=out_sh, gate_sh=gate_sh, up_sh=up_sh, down_sh=down_sh,
    )
    outputs = dict(
        block_out=(half, depth),
        grad_tokens=(half, depth),
        o_small=(8, depth),
        o_in=(3, rows, channels),
        o_out=(rows, channels),
        o_gate=(rows, units),
        o_up=(rows, units),
        o_down=(rows, units),
    )
    io = 3 * channels + channels
    flows = 12
    scratch = dict(
        in_full=vmem((3, ranks, rows, channels), BF16),
        out_full=vmem((ranks, rows, channels), BF16),
        gate_full=vmem((ranks, rows, units), BF16),
        up_full=vmem((ranks, rows, units), BF16),
        down_full=vmem((ranks, rows, units), BF16),
        grad_down=vmem((ranks, rows, units), BF16),
        theirs_down=vmem((chips, rows, units), BF16),
        theirs_gate=vmem((chips, rows, units), BF16),
        theirs_up=vmem((chips, rows, units), BF16),
        theirs_io=vmem((chips, rows, io), BF16),
        moving_down=vmem((chips - 1, rows, units), BF16),
        moving_gate=vmem((chips - 1, rows, units), BF16),
        moving_up=vmem((chips - 1, rows, units), BF16),
        moving_io=vmem((chips - 1, rows, io), BF16),
        rows_one=vmem((full, depth), BF16),
        cot_rows=vmem((full, depth), BF16),
        rows_two=vmem((full, depth), BF16),
        resid_rows=vmem((full, depth), BF16),
        across_t=vmem((depth, full), BF16),
        projected=vmem((3, full, channels), F32),
        conv_out=vmem((full, channels), F32),
        gated=vmem((full, channels), BF16),
        acc=vmem((half, depth), F32),
        resid=vmem((half, depth), F32),
        hidden=vmem((full, units), BF16),
        activ=vmem((full, units), F32),
        slope=vmem((full, units), F32),
        back_gate=vmem((full, units), BF16),
        back_up=vmem((full, units), BF16),
        back_proj=vmem((3, full, channels), BF16),
        small=vmem((8, depth), F32),
        small_pair=vmem((8, depth), F32),
        smalls=vmem((chips, 8, depth), F32),
        folded=vmem((8, depth), F32),
        folded_other=vmem((8, depth), F32),
        **{f"away{k}": vmem((half, depth), BF16) for k in range(4)},
        **{f"near{k}": vmem((half, depth), BF16) for k in range(4)},
        **{f"g_{k}": dma((flows, chips)) for k in ("send", "recv", "hand", "take")},
        **{f"s_{k}": dma((flows, chips)) for k in ("send", "recv", "hand", "take") if chips <= 16},
        g_own=dma((flows,)),
        x_send=dma((9,)),
        x_recv=dma((9,)),
        m_send=dma((chips - 1,)),
        m_recv=dma((chips - 1,)),
        m_pair=dma((2,)),
        o_sem=dma((7,)),
    )
    here = {"in_sh", "out_sh", "gate_sh", "up_sh", "down_sh", "o_in", "o_out", "o_gate", "o_up", "o_down"}

    def spec(name):
        return pl.BlockSpec(memory_space=pl.ANY if name in here else pltpu.VMEM)

    names = tuple(inputs) + tuple(outputs) + tuple(scratch)
    dims = (chips, ranks, rows, depth, channels, units, half)
    return pl.pallas_call(
        functools.partial(block_kernel, dims, names),
        out_shape=[jax.ShapeDtypeStruct(shape, F32) for shape in outputs.values()],
        in_specs=[spec(name) for name in inputs],
        out_specs=[spec(name) for name in outputs],
        scratch_shapes=list(scratch.values()),
        compiler_params=pltpu.CompilerParams(
            collective_id=1, has_side_effects=True, vmem_limit_bytes=67043328
        ),
    )(*inputs.values())


def reset_masks(segment):
    padded = jnp.concatenate([jnp.full((2,), -1, segment.dtype), segment])
    same_one, same_two = segment == padded[1:-1], segment == padded[:-2]
    masks = jnp.stack([same_one, same_two]).astype(F32)
    half = segment.shape[0] // 2
    turned = jnp.concatenate([masks[:, half:], masks[:, :half]], axis=1)
    masks = jnp.where(lax.axis_index("tensor") == 0, masks, turned)
    return jnp.broadcast_to(masks[:, :, None], masks.shape + (128,))


def local(
    tokens,
    segment_ids,
    norm1_gain,
    in_proj,
    conv_weight,
    out_proj,
    norm2_gain,
    gate_up,
    down_proj,
    cotangent,
    *,
    ranks,
):
    block_out, grad_tokens, small, grad_in, grad_out, grad_gate, grad_up, grad_down = run_block(
        tokens,
        cotangent,
        reset_masks(segment_ids[0]),
        conv_weight,
        norm1_gain[None],
        norm2_gain[None],
        in_proj.transpose(1, 0, 2),
        out_proj,
        gate_up[:, 0, :],
        gate_up[:, 1, :],
        down_proj,
        ranks,
    )
    return (
        block_out,
        grad_tokens,
        small[0],
        grad_in.transpose(1, 0, 2),
        small[2:5],
        grad_out,
        small[1],
        jnp.stack([grad_gate, grad_up], axis=1),
        grad_down,
    )


def solution(mesh):
    placed = (
        P(("dp", "tensor"), None),
        P("dp", None),
        P(),
        P("dp", None, "tensor"),
        P(),
        P("dp", "tensor"),
        P(),
        P("dp", None, "tensor"),
        P("dp", "tensor"),
        P(("dp", "tensor"), None),
    )
    return jax.shard_map(
        functools.partial(local, ranks=mesh.shape["dp"]),
        mesh=mesh,
        in_specs=placed,
        out_specs=(
            P(("dp", "tensor"), None),
            P(("dp", "tensor"), None),
            P(),
            P("dp", None, "tensor"),
            P(),
            P("dp", "tensor"),
            P(),
            P("dp", None, "tensor"),
            P("dp", "tensor"),
        ),
        check_vma=False,
    )
```
